32 devices in a mesh: dp: 8 (over z, y), mp: 4 (over x, core).
Axes of the slice: x: 2, y: 2, z: 4, core: 2. Of those that a mesh axis runs over, the one named last changes fastest.
Arguments:
- query: bfloat16 [4096, 4096], P('dp', 'mp'), may hold values from -6 to 6
- passage: bfloat16 [4096, 4096], P('dp', 'mp'), may hold values from -6 to 6
- query_scale: bfloat16 [4096], P('dp'), may hold values from 0.4 to 2.5
- passage_scale: bfloat16 [4096], P('dp'), may hold values from 0.4 to 2.5
- partners: int32 [8, 3], P('dp'), may hold values from 0 to 3, as said below
- counts: int32 [8], replicated, may hold values from 256 to 512, as said below
Outputs:
- loss: float32 [], replicated
- grad_query: bfloat16 [4096, 4096], P('dp', 'mp')
- grad_passage: bfloat16 [4096, 4096], P('dp', 'mp')
The draws below stay inside these ranges and needn't reach their ends.
Inputs may be any that keep to these rules, and one draw needn't show every extreme that they name: `partners`: each nonzero entry of a row is a distinct distance; block 0 and the last 3 blocks use all 3 slots. `counts`: some block has all 512 rows valid.
All inputs are finite; a program needn't handle non-finite values.
Results may differ from the reference program's by a relative error of at most 0.004.
Values may be sent and summed in bfloat16 or wider, within the bound.
A program may use at most 64 MiB of HBM per device.

```python
import math
import jax
import jax.numpy as jnp
from jax import lax

D = 4096
BLOCK = 512
WIN = 3
PMAX = 3
BLOCKS = 8
ROWS = 4096


def embed_all(key):
    key_q = jax.random.fold_in(key, 101)
    key_p = jax.random.fold_in(key, 102)
    key_a = jax.random.fold_in(key, 104)
    key_b = jax.random.fold_in(key, 105)
    values_q = jnp.clip(jax.random.normal(key_q, (ROWS, D), jnp.float32), -6.0, 6.0)
    values_p = jnp.clip(jax.random.normal(key_p, (ROWS, D), jnp.float32), -6.0, 6.0)
    scale_q = jnp.exp(jax.random.uniform(key_a, (ROWS,), jnp.float32, math.log(0.5), math.log(2.0)))
    scale_p = jnp.exp(jax.random.uniform(key_b, (ROWS,), jnp.float32, math.log(0.5), math.log(2.0)))
    return (values_q, values_p, scale_q, scale_p)


def draw_query(key, part):
    return embed_all(key)[0].astype(jnp.bfloat16)


def draw_passage(key, part):
    return embed_all(key)[1].astype(jnp.bfloat16)


def draw_query_scale(key, part):
    return embed_all(key)[2].astype(jnp.bfloat16)


def draw_passage_scale(key, part):
    return embed_all(key)[3].astype(jnp.bfloat16)


def draw_partners(key, part):
    key_c = jax.random.fold_in(key, 201)
    key_o = jax.random.fold_in(key, 202)
    used = jax.random.randint(key_c, (BLOCKS,), 0, PMAX + 1)
    block_ids = jnp.arange(BLOCKS)
    forced = (block_ids == 0) | (block_ids >= BLOCKS - WIN)
    used = jnp.where(forced, PMAX, used)
    ranks = jax.random.randint(key_o, (BLOCKS, WIN), 0, 1 << 20) * WIN + jnp.arange(WIN)[None, :]
    order = jnp.argsort(ranks, axis=1)[:, :PMAX] + 1
    slot = jnp.arange(PMAX)[None, :]
    return jnp.where(slot < used[:, None], order, 0).astype(jnp.int32)


def draw_counts(key, part):
    key_c = jax.random.fold_in(key, 301)
    key_f = jax.random.fold_in(key, 302)
    values = jax.random.randint(key_c, (BLOCKS,), BLOCK // 2, BLOCK + 1)
    full = jax.random.randint(key_f, (), 0, BLOCKS)
    return jnp.where(jnp.arange(BLOCKS) == full, BLOCK, values).astype(jnp.int32)


def setup_inputs(seed: int = 0) -> dict:
    keys = jax.random.split(jax.random.key(seed), 7)
    query = draw_query(jax.random.fold_in(keys[6], 71), 0)
    passage = draw_passage(jax.random.fold_in(keys[6], 71), 0)
    query_scale = draw_query_scale(jax.random.fold_in(keys[6], 71), 0)
    passage_scale = draw_passage_scale(jax.random.fold_in(keys[6], 71), 0)
    partners = draw_partners(jax.random.fold_in(keys[6], 71), 0)
    counts = draw_counts(jax.random.fold_in(keys[6], 71), 0)
    return dict(query=query, passage=passage, query_scale=query_scale, passage_scale=passage_scale, partners=partners, counts=counts)


def reference(query, passage, query_scale, passage_scale, partners, counts):
    inv = 1.0 / math.sqrt(D)
    q3 = query.reshape(BLOCKS, BLOCK, D)
    p3 = passage.reshape(BLOCKS, BLOCK, D)
    qs3 = query_scale.astype(jnp.float32).reshape(BLOCKS, BLOCK)
    ps3 = passage_scale.astype(jnp.float32).reshape(BLOCKS, BLOCK)
    column = jnp.arange(BLOCK, dtype=jnp.int32)

    def make_tile(a, b):
        raw = jnp.dot(q3[a], p3[b].T, preferred_element_type=jnp.float32)
        return raw * (qs3[a] * inv)[:, None] * ps3[b][None, :]

    def forward(a):
        offs = partners[a]
        blocks = jnp.concatenate([a[None], (a + offs) % BLOCKS]).astype(jnp.int32)
        live = jnp.concatenate([jnp.array([True]), offs > 0])
        scores = jnp.stack([make_tile(a, blocks[k]) for k in range(1 + PMAX)])
        col_ok = live[:, None] & (column[None, :] < counts[blocks][:, None])
        masked = jnp.where(col_ok[:, None, :], scores, -jnp.inf)
        top = lax.optimization_barrier(jnp.max(masked, axis=(0, 2)))
        weights = jnp.exp(masked - top[None, :, None])
        total = lax.optimization_barrier(jnp.sum(weights, axis=(0, 2)))
        lse = top + jnp.log(total)
        valid = column < counts[a]
        positive = jnp.diagonal(scores[0])
        loss_sum = jnp.sum(jnp.where(valid, lse - positive, 0.0))
        grads = weights / total[None, :, None]
        target = (column[:, None] == column[None, :]).astype(jnp.float32)
        grads = jnp.concatenate([(grads[0] - target)[None], grads[1:]])
        grads = jnp.where(valid[None, :, None], grads, 0.0)
        key_weight = (grads * ps3[blocks][:, None, :]).astype(jnp.bfloat16)
        gq = jnp.zeros((BLOCK, D), jnp.float32)
        for k in range(1 + PMAX):
            gq = gq + jnp.dot(key_weight[k], p3[blocks[k]], preferred_element_type=jnp.float32)
        return (lse, loss_sum, gq.astype(jnp.bfloat16))
    lses, losses, gqs = lax.map(forward, jnp.arange(BLOCKS, dtype=jnp.int32))

    def backward(b):
        col_ok = column < counts[b]
        scores = make_tile(b, b)
        masked = jnp.where(col_ok[None, :], scores, -jnp.inf)
        grads = jnp.exp(masked - lses[b][:, None])
        grads = grads - (column[:, None] == column[None, :]).astype(jnp.float32)
        grads = jnp.where((column < counts[b])[:, None] & col_ok[None, :], grads, 0.0)
        row_weight = (grads * qs3[b][:, None]).astype(jnp.bfloat16)
        total = jnp.dot(row_weight.T, q3[b], preferred_element_type=jnp.float32)
        for offset in range(1, WIN + 1):
            a = ((b - offset) % BLOCKS).astype(jnp.int32)
            live = jnp.any(partners[a] == offset)
            scores = make_tile(a, b)
            masked = jnp.where(col_ok[None, :] & live, scores, -jnp.inf)
            grads = jnp.exp(masked - lses[a][:, None])
            grads = jnp.where((column < counts[a])[:, None], grads, 0.0)
            row_weight = (grads * qs3[a][:, None]).astype(jnp.bfloat16)
            part = jnp.dot(row_weight.T, q3[a], preferred_element_type=jnp.float32).astype(jnp.bfloat16)
            total = total + lax.optimization_barrier(part).astype(jnp.float32)
        return total.astype(jnp.bfloat16)
    gps = lax.map(backward, jnp.arange(BLOCKS, dtype=jnp.int32))
    loss = jnp.sum(losses) / jnp.sum(counts).astype(jnp.float32)
    return (loss, gqs.reshape(ROWS, D), gps.reshape(ROWS, D))
```

```python
import functools
import math

import jax
import jax.numpy as jnp
from jax import lax
from jax.experimental import pallas as pl
from jax.experimental.pallas import tpu as pltpu
from jax.sharding import PartitionSpec as P

WIN = 3
CHUNKS = 4
GROUP = 32
MESH = pl.DeviceIdType.MESH


def kernel(ndp, nmp, inv, q_ref, p_ref, ps_ref, qs_ref, ok_ref, bias_ref,
           gq_ref, gp_ref, loss_ref,
           pbuf, qbuf, psbuf, raw, inbox, weights, rw_out, rw_in, acc, lsum, lin,
           p_ss, p_rs, q_ss, q_rs, sc_ss, sc_rs, t_ss, t_rs, k_ss, k_rs,
           d_ss, d_rs, g_ss, g_rs, l_ss, l_rs):
    d = lax.axis_index("dp")
    m = lax.axis_index("mp")
    rows, width = q_ref.shape
    share = rows // nmp
    step = rows // CHUNKS

    def at_dp(delta):
        return (lax.rem(d + delta + ndp, ndp), m)

    def at_mp(delta):
        return (d, lax.rem(m + delta, nmp))

    def flip(index, bit):
        return index + bit - 2 * bit * lax.rem(index // bit, 2)

    def rows_of(block):
        return pl.ds(pl.multiple_of(block * share, share), share)

    even = lax.rem(d, 2) == 0
    odd = lax.rem(d, 2) == 1
    partner = (flip(d, 1), m)
    mp_bits = [1 << b for b in range(nmp.bit_length() - 1)]
    dp_bits = [1 << b for b in range(ndp.bit_length() - 1)]

    peers = [at_dp(s * k) for k in range(1, WIN + 1) for s in (1, -1)]
    peers += [at_mp(j) for j in range(1, nmp)]
    peers += [(flip(d, b), m) for b in dp_bits if b > WIN]
    barrier = pltpu.get_barrier_semaphore()
    for peer in peers:
        pl.semaphore_signal(barrier, inc=1, device_id=peer, device_id_type=MESH)
    pl.semaphore_wait(barrier, len(peers))

    def copy(src, dst, ssem, rsem, dev):
        return pltpu.make_async_remote_copy(
            src_ref=src, dst_ref=dst, send_sem=ssem, recv_sem=rsem,
            device_id=dev, device_id_type=MESH)

    class Stream:
        def __init__(self, own, buf, ss, rs, dest):
            self.own, self.buf, self.ss, self.rs, self.dest = own, buf, ss, rs, dest

        def cut(self, c):
            return pl.ds(c * step, step)

        def direct(self, c):
            s = self.cut(c)
            return copy(self.own.at[s], self.buf.at[1, s], self.ss.at[0, c], self.rs.at[1, c], self.dest)

        def near_relay(self, c):
            s = self.cut(c)
            return copy(self.buf.at[1, s], self.buf.at[0, s], self.ss.at[1, c], self.rs.at[0, c], partner)

        def near_own(self, c):
            s = self.cut(c)
            return copy(self.own.at[s], self.buf.at[0, s], self.ss.at[1, c], self.rs.at[0, c], partner)

        def far_near(self, c):
            s = self.cut(c)
            return copy(self.buf.at[1, s], self.buf.at[2, s], self.ss.at[2, c], self.rs.at[2, c], partner)

        def far_next(self, c):
            s = self.cut(c)
            return copy(self.buf.at[0, s], self.buf.at[2, s], self.ss.at[3, c], self.rs.at[2, c], self.dest)

        def arrived(self, slot, c):
            s = self.cut(c)
            copy(self.buf.at[slot, s], self.buf.at[slot, s], self.ss.at[0, c], self.rs.at[slot, c], partner).wait_recv()

        def start_own(self, is_b):
            for c in range(CHUNKS):
                self.direct(c).start()

            @pl.when(is_b)
            def _():
                for c in range(CHUNKS):
                    self.near_own(c).start()

        def relay_two(self, is_b):
            for c in range(CHUNKS):
                self.arrived(1, c)

                @pl.when(is_b)
                def _():
                    self.far_near(c).start()

                @pl.when(jnp.logical_not(is_b))
                def _():
                    self.near_relay(c).start()

        def relay_one(self, is_b):
            for c in range(CHUNKS):
                self.arrived(0, c)

                @pl.when(is_b)
                def _():
                    self.far_next(c).start()

        def relay_all(self, is_b):
            for c in range(CHUNKS):
                self.arrived(1, c)

                @pl.when(is_b)
                def _():
                    self.far_near(c).start()
                    self.arrived(0, c)
                    self.far_next(c).start()

                @pl.when(jnp.logical_not(is_b))
                def _():
                    self.near_relay(c).start()
                    self.arrived(0, c)

        def finish(self, is_b):
            for c in range(CHUNKS):
                self.direct(c).wait_send()

                @pl.when(is_b)
                def _():
                    self.near_own(c).wait_send()
                    self.far_near(c).wait_send()
                    self.far_next(c).wait_send()

                @pl.when(jnp.logical_not(is_b))
                def _():
                    self.near_relay(c).wait_send()

    ps = Stream(p_ref, pbuf, p_ss, p_rs, at_dp(-2))
    qs = Stream(q_ref, qbuf, q_ss, q_rs, at_dp(2))

    def scale_copy(k):
        return copy(ps_ref, psbuf.at[k - 1], sc_ss.at[k - 1], sc_rs.at[k - 1], at_dp(-k))

    for k in range(1, WIN + 1):
        scale_copy(k).start()
    ps.start_own(odd)

    def tile_copy(k, j):
        return copy(raw.at[k, rows_of(lax.rem(m + j, nmp))], inbox.at[j - 1, k],
                    t_ss.at[j - 1, k], t_rs.at[j - 1, k], at_mp(j))

    def tile(k):
        keys = p_ref if k == 0 else pbuf.at[k - 1]

        @pl.loop(0, nmp)
        def _(r):
            at = rows_of(r)
            raw[k, at, :] = lax.dot_general(
                q_ref[at, :], keys[...], (((1,), (1,)), ((), ())),
                preferred_element_type=jnp.float32)
        for j in range(1, nmp):
            tile_copy(k, j).start()

    tile(0)
    ps.relay_two(odd)
    qs.start_own(even)
    ps.relay_one(odd)
    tile(2)
    tile(1)
    qs.relay_two(even)
    for c in range(CHUNKS):
        ps.arrived(2, c)
    tile(3)
    for k in range(1, WIN + 1):
        scale_copy(k).wait_recv()
    for k in (0, 2, 1, 3):
        for j in range(1, nmp):
            tile_copy(k, j).wait_recv()

    lsum[...] = jnp.zeros_like(lsum)

    @pl.loop(0, share // GROUP)
    def _(g):
        low = pl.multiple_of(g * GROUP, GROUP)
        here = pl.ds(low, GROUP)
        whole = pl.ds(pl.multiple_of(m * share + low, GROUP), GROUP)
        row_scale = qs_ref[whole, :]
        valid = ok_ref[whole, :] > 0.0
        cols = lax.broadcasted_iota(jnp.int32, (GROUP, rows), 1)
        ids = lax.broadcasted_iota(jnp.int32, (GROUP, rows), 0) + (m * share + low)
        diagonal = cols == ids
        key_scale = [ps_ref[0:1, :]] + [psbuf[k, 0:1, :] for k in range(WIN)]
        scores = []
        for k in range(WIN + 1):
            s = raw[k, whole, :]
            for j in range(nmp - 1):
                s = s + inbox[j, k, here, :]
            scores.append(s * (row_scale * inv) * key_scale[k])
        masked = [scores[k] + bias_ref[k:k + 1, :] for k in range(WIN + 1)]
        top = functools.reduce(jnp.maximum, [jnp.max(x, axis=1, keepdims=True) for x in masked])
        exps = [jnp.exp(x - top) for x in masked]
        total = sum(jnp.sum(x, axis=1, keepdims=True) for x in exps)
        lse = top + jnp.log(total)
        positive = jnp.sum(jnp.where(diagonal, scores[0], 0.0), axis=1, keepdims=True)
        lost = jnp.sum(jnp.where(valid, lse - positive, 0.0), axis=0, keepdims=True)
        lsum[0] = lsum[0] + lost
        for k in range(WIN + 1):
            grad = exps[k] / total
            if k == 0:
                grad = grad - diagonal.astype(jnp.float32)
            grad = jnp.where(valid, grad, 0.0)
            weights[k, whole, :] = (grad * key_scale[k]).astype(jnp.bfloat16)
            if k == 0:
                weights[WIN + 1, whole, :] = (grad * row_scale).astype(jnp.bfloat16)
            else:
                rw_out[k - 1, here, :] = (grad * row_scale).astype(jnp.bfloat16)

    def dispatch(k):
        return copy(rw_out.at[k - 1], rw_in.at[k - 1, rows_of(m)], d_ss.at[k - 1], d_rs.at[k - 1], at_dp(k))

    for k in range(1, WIN + 1):
        dispatch(k).start()

    class Gather:
        def __init__(self, buf, ss, rs):
            self.buf, self.ss, self.rs = buf, ss, rs
            known = [0]
            self.steps = []
            for bit in reversed(mp_bits):
                self.steps += [(s, bit) for s in known]
                known = known + [s ^ bit for s in known]
            self.steps.sort(key=lambda t: t[0])
            self.got = set()

        def hop(self, s, bit):
            block = m
            for b in mp_bits:
                if s & b:
                    block = flip(block, b)
            part = self.buf.at[:, rows_of(block)]
            return copy(part, part, self.ss.at[s ^ bit], self.rs.at[s ^ bit], (d, flip(m, bit)))

        def take(self, s):
            if s and s not in self.got:
                self.got.add(s)
                block = m
                for b in mp_bits:
                    if s & b:
                        block = flip(block, b)
                part = self.buf.at[:, rows_of(block)]
                copy(part, part, self.ss.at[s], self.rs.at[s], (d, flip(m, 1))).wait_recv()

        def begin(self):
            for s, bit in self.steps:
                if s == 0:
                    self.hop(s, bit).start()

        def rest(self):
            for s, bit in self.steps:
                if s:
                    self.take(s)
                    self.hop(s, bit).start()

        def all(self):
            for s in range(1, nmp):
                self.take(s)

        def finish(self):
            for s, bit in self.steps:
                self.hop(s, bit).wait_send()

    local = Gather(weights, k_ss, k_rs)
    foreign = Gather(rw_in, g_ss, g_rs)
    local.begin()
    qs.relay_one(even)
    for k in range(1, WIN + 1):
        dispatch(k).wait_recv()
    foreign.begin()
    local.rest()
    local.all()
    foreign.rest()

    @pl.loop(0, nmp)
    def _(r):
        at = rows_of(r)
        out = jnp.dot(weights[0, at, :], p_ref[...], preferred_element_type=jnp.float32)
        for k in range(WIN):
            out = out + jnp.dot(weights[k + 1, at, :], pbuf[k], preferred_element_type=jnp.float32)
        gq_ref[at, :] = out.astype(jnp.bfloat16)

    def back(w, x):
        return lax.dot_general(w, x, (((0,), (0,)), ((), ())), preferred_element_type=jnp.float32)

    stages = [(d, flip(m, b)) for b in mp_bits] + [(flip(d, b), m) for b in dp_bits]

    def loss_copy(i):
        return copy(lsum.at[i], lin.at[i], l_ss.at[i], l_rs.at[i], stages[i])

    for i in range(len(stages)):
        loss_copy(i).start()
        loss_copy(i).wait_recv()
        lsum[i + 1] = lsum[i] + lin[i]
    loss_ref[...] = lsum[len(stages)]

    for c in range(CHUNKS):
        qs.arrived(2, c)
    foreign.all()
    jc = 128

    @pl.loop(0, rows // jc)
    def _(t):
        at = pl.ds(pl.multiple_of(t * jc, jc), jc)
        out = back(weights[WIN + 1, :, at], q_ref[...])
        for k in range(WIN):
            out = out + back(rw_in[k, :, at], qbuf[k])
        gp_ref[at, :] = out.astype(jnp.bfloat16)

    ps.finish(odd)
    qs.finish(even)
    for k in range(1, WIN + 1):
        scale_copy(k).wait_send()
        dispatch(k).wait_send()
    for k in range(WIN + 1):
        for j in range(1, nmp):
            tile_copy(k, j).wait_send()
    local.finish()
    foreign.finish()
    for i in range(len(stages)):
        loss_copy(i).wait_send()


def local(ndp, nmp, query, passage, query_scale, passage_scale, partners, counts):
    rows, width = query.shape
    inv = 1.0 / math.sqrt(width * nmp)
    share = rows // nmp
    mine = lax.axis_index("dp")
    ids = jnp.arange(counts.shape[0], dtype=jnp.int32)
    offsets = jnp.arange(WIN + 1, dtype=jnp.int32)
    near = (mine + offsets) % ndp
    key_counts = jnp.sum(jnp.where(ids[None, :] == near[:, None], counts[None, :], 0), axis=1)
    live = (offsets == 0) | jnp.any(partners[0][None, :] == offsets[:, None], axis=1)
    column = jnp.arange(rows, dtype=jnp.int32)
    bias = jnp.where(live[:, None] & (column[None, :] < key_counts[:, None]), 0.0, -jnp.inf).astype(jnp.float32)
    ok = (column < key_counts[0]).astype(jnp.float32)[:, None]
    ps = jnp.broadcast_to(passage_scale.astype(jnp.float32)[None, :], (8, rows))
    qs = query_scale.astype(jnp.float32)[:, None]
    nst = (ndp * nmp).bit_length() - 1
    bf, f32 = jnp.bfloat16, jnp.float32
    dma = pltpu.SemaphoreType.DMA
    vm = pl.BlockSpec(memory_space=pltpu.VMEM)
    gq, gp, loss = pl.pallas_call(
        functools.partial(kernel, ndp, nmp, inv),
        out_shape=[
            jax.ShapeDtypeStruct((rows, width), bf),
            jax.ShapeDtypeStruct((rows, width), bf),
            jax.ShapeDtypeStruct((8, 128), f32),
        ],
        in_specs=[vm] * 6,
        out_specs=[vm] * 3,
        scratch_shapes=[
            pltpu.VMEM((WIN, rows, width), bf),
            pltpu.VMEM((WIN, rows, width), bf),
            pltpu.VMEM((WIN, 8, rows), f32),
            pltpu.VMEM((WIN + 1, rows, rows), f32),
            pltpu.VMEM((nmp - 1, WIN + 1, share, rows), f32),
            pltpu.VMEM((WIN + 2, rows, rows), bf),
            pltpu.VMEM((WIN, share, rows), bf),
            pltpu.VMEM((WIN, rows, rows), bf),
            pltpu.VMEM((8, 128), f32),
            pltpu.VMEM((nst + 1, 8, 128), f32),
            pltpu.VMEM((nst, 8, 128), f32),
            dma((4, CHUNKS)), dma((WIN, CHUNKS)),
            dma((4, CHUNKS)), dma((WIN, CHUNKS)),
            dma((WIN,)), dma((WIN,)),
            dma((nmp - 1, WIN + 1)), dma((nmp - 1, WIN + 1)),
            dma((nmp,)), dma((nmp,)),
            dma((WIN,)), dma((WIN,)),
            dma((nmp,)), dma((nmp,)),
            dma((nst,)), dma((nst,)),
        ],
        compiler_params=pltpu.CompilerParams(
            collective_id=0, has_side_effects=True, vmem_limit_bytes=56 * 1024 * 1024),
    )(query, passage, ps, qs, ok, bias)
    return loss[0, 0] / jnp.sum(counts).astype(f32), gq, gp


def solution(mesh):
    return jax.shard_map(
        functools.partial(local, mesh.shape["dp"], mesh.shape["mp"]),
        mesh=mesh,
        in_specs=(P("dp", "mp"), P("dp", "mp"), P("dp"), P("dp"), P("dp", None), P()),
        out_specs=(P(), P("dp", "mp"), P("dp", "mp")),
        check_vma=False,
    )
```

```python
import functools
import math

import jax
import jax.numpy as jnp
from jax import lax
from jax.experimental import pallas as pl
from jax.experimental.pallas import tpu as pltpu
from jax.sharding import PartitionSpec as P

WIN = 3
CHUNKS = 4
GROUP = 32
MESH = pl.DeviceIdType.MESH


def kernel(ndp, nmp, inv, q_ref, p_ref, ps_ref, qs_ref, meta_ref,
           gq_ref, gp_ref, loss_ref,
           pbuf, qbuf, psbuf, raw, inbox, weights, rw_out, rw_in, lsum, lin,
           p_ss, p_rs, q_ss, q_rs, sc_ss, sc_rs, t_ss, t_rs, k_ss, k_rs,
           d_ss, d_rs, g_ss, g_rs, l_ss, l_rs):
    d = lax.axis_index("dp")
    m = lax.axis_index("mp")
    rows, width = q_ref.shape
    share = rows // nmp
    step = rows // CHUNKS

    def at_dp(delta):
        return (lax.rem(d + delta + ndp, ndp), m)

    def at_mp(delta):
        return (d, lax.rem(m + delta, nmp))

    def flip(index, bit):
        return index + bit - 2 * bit * lax.rem(index // bit, 2)

    def rows_of(block):
        return pl.ds(pl.multiple_of(block * share, share), share)

    even = lax.rem(d, 2) == 0
    odd = lax.rem(d, 2) == 1
    partner = (flip(d, 1), m)
    mp_bits = [1 << b for b in range(nmp.bit_length() - 1)]
    dp_bits = [1 << b for b in range(ndp.bit_length() - 1)]

    peers = [at_dp(s * k) for k in range(1, WIN + 1) for s in (1, -1)]
    peers += [at_mp(j) for j in range(1, nmp)]
    peers += [(flip(d, b), m) for b in dp_bits if b > WIN]
    barrier = pltpu.get_barrier_semaphore()
    for peer in peers:
        pl.semaphore_signal(barrier, inc=1, device_id=peer, device_id_type=MESH)
    pl.semaphore_wait(barrier, len(peers))

    def copy(src, dst, ssem, rsem, dev):
        return pltpu.make_async_remote_copy(
            src_ref=src, dst_ref=dst, send_sem=ssem, recv_sem=rsem,
            device_id=dev, device_id_type=MESH)

    class Stream:
        def __init__(self, own, buf, ss, rs, dest):
            self.own, self.buf, self.ss, self.rs, self.dest = own, buf, ss, rs, dest

        def cut(self, c):
            return pl.ds(c * step, step)

        def direct(self, c):
            s = self.cut(c)
            return copy(self.own.at[s], self.buf.at[1, s], self.ss.at[0, c], self.rs.at[1, c], self.dest)

        def near_relay(self, c):
            s = self.cut(c)
            return copy(self.buf.at[1, s], self.buf.at[0, s], self.ss.at[1, c], self.rs.at[0, c], partner)

        def near_own(self, c):
            s = self.cut(c)
            return copy(self.own.at[s], self.buf.at[0, s], self.ss.at[1, c], self.rs.at[0, c], partner)

        def far_near(self, c):
            s = self.cut(c)
            return copy(self.buf.at[1, s], self.buf.at[2, s], self.ss.at[2, c], self.rs.at[2, c], partner)

        def far_next(self, c):
            s = self.cut(c)
            return copy(self.buf.at[0, s], self.buf.at[2, s], self.ss.at[3, c], self.rs.at[2, c], self.dest)

        def arrived(self, slot, c):
            s = self.cut(c)
            copy(self.buf.at[slot, s], self.buf.at[slot, s], self.ss.at[0, c], self.rs.at[slot, c], partner).wait_recv()

        def start_own(self, is_b):
            for c in range(CHUNKS):
                self.direct(c).start()

            @pl.when(is_b)
            def _():
                for c in range(CHUNKS):
                    self.near_own(c).start()

        def relay_two(self, is_b):
            for c in range(CHUNKS):
                self.arrived(1, c)

                @pl.when(is_b)
                def _():
                    self.far_near(c).start()

                @pl.when(jnp.logical_not(is_b))
                def _():
                    self.near_relay(c).start()

        def relay_one(self, is_b):
            for c in range(CHUNKS):
                self.arrived(0, c)

                @pl.when(is_b)
                def _():
                    self.far_next(c).start()

        def relay_all(self, is_b):
            for c in range(CHUNKS):
                self.arrived(1, c)

                @pl.when(is_b)
                def _():
                    self.far_near(c).start()
                    self.arrived(0, c)
                    self.far_next(c).start()

                @pl.when(jnp.logical_not(is_b))
                def _():
                    self.near_relay(c).start()
                    self.arrived(0, c)

        def finish(self, is_b):
            for c in range(CHUNKS):
                self.direct(c).wait_send()

                @pl.when(is_b)
                def _():
                    self.near_own(c).wait_send()
                    self.far_near(c).wait_send()
                    self.far_next(c).wait_send()

                @pl.when(jnp.logical_not(is_b))
                def _():
                    self.near_relay(c).wait_send()

    ps = Stream(p_ref, pbuf, p_ss, p_rs, at_dp(-2))
    qs = Stream(q_ref, qbuf, q_ss, q_rs, at_dp(2))

    def scale_copy(k):
        return copy(ps_ref, psbuf.at[k - 1], sc_ss.at[k - 1], sc_rs.at[k - 1], at_dp(-k))

    for k in range(1, WIN + 1):
        scale_copy(k).start()
    ps.start_own(odd)

    def across(s):
        block = m
        for b in mp_bits:
            if s & b:
                block = flip(block, b)
        return rows_of(block)

    def tile_copy(k, s):
        return copy(raw.at[k, across(s)], inbox.at[s - 1, k],
                    t_ss.at[s - 1, k], t_rs.at[s - 1, k], (d, flip(m, s & -s)))

    def tile_next(k):
        for bit in mp_bits[1:]:
            for s in range(bit, nmp, 2 * bit):
                for b in mp_bits:
                    if b < bit:
                        tile_copy(k, s | b).wait_recv()
                        raw[k, across(s), :] += inbox[(s | b) - 1, k]
                tile_copy(k, s).start()

    def tile(k):
        keys = p_ref if k == 0 else pbuf.at[k - 1]

        @pl.loop(0, nmp)
        def _(r):
            at = rows_of(r)
            raw[k, at, :] = lax.dot_general(
                q_ref[at, :], keys[...], (((1,), (1,)), ((), ())),
                preferred_element_type=jnp.float32)
        for s in range(1, nmp, 2):
            tile_copy(k, s).start()

    tile(0)
    tile_next(0)
    ps.relay_two(odd)
    qs.start_own(even)
    ps.relay_one(odd)
    tile(2)
    tile(1)
    tile_next(2)
    tile_next(1)
    qs.relay_two(even)
    for c in range(CHUNKS):
        ps.arrived(2, c)
    tile(3)
    tile_next(3)
    for k in range(1, WIN + 1):
        scale_copy(k).wait_recv()
    for k in (0, 2, 1, 3):
        for b in mp_bits:
            tile_copy(k, b).wait_recv()

    lsum[...] = jnp.zeros_like(lsum)

    @pl.loop(0, share // GROUP)
    def _(g):
        low = pl.multiple_of(g * GROUP, GROUP)
        here = pl.ds(low, GROUP)
        whole = pl.ds(pl.multiple_of(m * share + low, GROUP), GROUP)
        row_scale = qs_ref[whole, :]
        cols = lax.broadcasted_iota(jnp.int32, (GROUP, rows), 1)
        ids = lax.broadcasted_iota(jnp.int32, (GROUP, rows), 0) + (m * share + low)
        diagonal = cols == ids
        valid = ids[:, 0:1] < meta_ref[0]
        key_scale = [ps_ref[0:1, :]] + [psbuf[k, 0:1, :] for k in range(WIN)]
        scores = []
        for k in range(WIN + 1):
            s = raw[k, whole, :]
            for b in mp_bits:
                s = s + inbox[b - 1, k, here, :]
            scores.append(s * (row_scale * inv) * key_scale[k])
        masked = [jnp.where(cols < meta_ref[k], scores[k], -jnp.inf) for k in range(WIN + 1)]
        top = functools.reduce(jnp.maximum, [jnp.max(x, axis=1, keepdims=True) for x in masked])
        exps = [jnp.exp(x - top) for x in masked]
        total = sum(jnp.sum(x, axis=1, keepdims=True) for x in exps)
        lse = top + jnp.log(total)
        positive = jnp.sum(jnp.where(diagonal, scores[0], 0.0), axis=1, keepdims=True)
        lost = jnp.sum(jnp.where(valid, lse - positive, 0.0), axis=0, keepdims=True)
        lsum[0] = lsum[0] + lost
        for k in range(WIN + 1):
            grad = exps[k] / total
            if k == 0:
                grad = grad - diagonal.astype(jnp.float32)
            grad = jnp.where(valid, grad, 0.0)
            weights[k, whole, :] = (grad * key_scale[k]).astype(jnp.bfloat16)
            if k == 0:
                weights[WIN + 1, whole, :] = (grad * row_scale).astype(jnp.bfloat16)
            else:
                rw_out[k - 1, here, :] = (grad * row_scale).astype(jnp.bfloat16)

    def dispatch(k):
        return copy(rw_out.at[k - 1], rw_in.at[k - 1, rows_of(m)], d_ss.at[k - 1], d_rs.at[k - 1], at_dp(k))

    for k in range(1, WIN + 1):
        dispatch(k).start()

    class Gather:
        def __init__(self, buf, ss, rs):
            self.buf, self.ss, self.rs = buf, ss, rs
            known = [0]
            self.steps = []
            for bit in reversed(mp_bits):
                self.steps += [(s, bit) for s in known]
                known = known + [s ^ bit for s in known]
            self.steps.sort(key=lambda t: t[0])
            self.got = set()

        def hop(self, s, bit):
            block = m
            for b in mp_bits:
                if s & b:
                    block = flip(block, b)
            part = self.buf.at[:, rows_of(block)]
            return copy(part, part, self.ss.at[s ^ bit], self.rs.at[s ^ bit], (d, flip(m, bit)))

        def take(self, s):
            if s and s not in self.got:
                self.got.add(s)
                block = m
                for b in mp_bits:
                    if s & b:
                        block = flip(block, b)
                part = self.buf.at[:, rows_of(block)]
                copy(part, part, self.ss.at[s], self.rs.at[s], (d, flip(m, 1))).wait_recv()

        def begin(self):
            for s, bit in self.steps:
                if s == 0:
                    self.hop(s, bit).start()

        def rest(self):
            for s, bit in self.steps:
                if s:
                    self.take(s)
                    self.hop(s, bit).start()

        def all(self):
            for s in range(1, nmp):
                self.take(s)

        def finish(self):
            for s, bit in self.steps:
                self.hop(s, bit).wait_send()

    local = Gather(weights, k_ss, k_rs)
    foreign = Gather(rw_in, g_ss, g_rs)
    stages = [(d, flip(m, b)) for b in mp_bits] + [(flip(d, b), m) for b in dp_bits]

    def loss_copy(i):
        return copy(lsum.at[i], lin.at[i], l_ss.at[i], l_rs.at[i], stages[i])

    def loss_step(i):
        if i:
            loss_copy(i - 1).wait_recv()
            lsum[i] = lsum[i - 1] + lin[i - 1]
        if i < len(stages):
            loss_copy(i).start()

    local.begin()
    loss_step(0)
    qs.relay_one(even)
    loss_step(1)
    for k in range(1, WIN + 1):
        dispatch(k).wait_recv()
    foreign.begin()
    loss_step(2)
    local.rest()
    loss_step(3)
    local.all()

    @pl.loop(0, nmp)
    def _(r):
        at = rows_of(r)
        out = jnp.dot(weights[0, at, :], p_ref[...], preferred_element_type=jnp.float32)
        for k in range(WIN):
            out = out + jnp.dot(weights[k + 1, at, :], pbuf[k], preferred_element_type=jnp.float32)
        gq_ref[at, :] = out.astype(jnp.bfloat16)

    loss_step(4)
    foreign.rest()
    def back(w, x):
        return lax.dot_general(w, x, (((0,), (0,)), ((), ())), preferred_element_type=jnp.float32)

    for c in range(CHUNKS):
        qs.arrived(2, c)
    foreign.all()
    for i in range(5, len(stages) + 1):
        loss_step(i)
    loss_ref[...] = lsum[len(stages), 0:1, 0:1] / meta_ref[WIN + 1].astype(jnp.float32)
    jc = 128

    @pl.loop(0, rows // jc)
    def _(t):
        at = pl.ds(pl.multiple_of(t * jc, jc), jc)
        out = back(weights[WIN + 1, :, at], q_ref[...])
        for k in range(WIN):
            out = out + back(rw_in[k, :, at], qbuf[k])
        gp_ref[at, :] = out.astype(jnp.bfloat16)

    ps.finish(odd)
    qs.finish(even)
    for k in range(1, WIN + 1):
        scale_copy(k).wait_send()
        dispatch(k).wait_send()
    for k in range(WIN + 1):
        for j in range(1, nmp):
            tile_copy(k, j).wait_send()
    local.finish()
    foreign.finish()
    for i in range(len(stages)):
        loss_copy(i).wait_send()


def local(ndp, nmp, query, passage, query_scale, passage_scale, partners, counts):
    rows, width = query.shape
    inv = 1.0 / math.sqrt(width * nmp)
    share = rows // nmp
    mine = lax.axis_index("dp")
    ids = jnp.arange(counts.shape[0], dtype=jnp.int32)
    offsets = jnp.arange(WIN + 1, dtype=jnp.int32)
    near = (mine + offsets) % ndp
    key_counts = jnp.sum(jnp.where(ids[None, :] == near[:, None], counts[None, :], 0), axis=1)
    live = (offsets == 0) | jnp.any(partners[0][None, :] == offsets[:, None], axis=1)
    meta = jnp.concatenate([jnp.where(live, key_counts, 0), jnp.sum(counts)[None]]).astype(jnp.int32)
    ps = jnp.broadcast_to(passage_scale.astype(jnp.float32)[None, :], (8, rows))
    qs = query_scale.astype(jnp.float32)[:, None]
    nst = (ndp * nmp).bit_length() - 1
    bf, f32 = jnp.bfloat16, jnp.float32
    dma = pltpu.SemaphoreType.DMA
    vm = pl.BlockSpec(memory_space=pltpu.VMEM)
    gq, gp, loss = pl.pallas_call(
        functools.partial(kernel, ndp, nmp, inv),
        out_shape=[
            jax.ShapeDtypeStruct((rows, width), bf),
            jax.ShapeDtypeStruct((rows, width), bf),
            jax.ShapeDtypeStruct((1, 1), f32),
        ],
        in_specs=[vm] * 4 + [pl.BlockSpec(memory_space=pltpu.SMEM)],
        out_specs=[vm] * 3,
        scratch_shapes=[
            pltpu.VMEM((WIN, rows, width), bf),
            pltpu.VMEM((WIN, rows, width), bf),
            pltpu.VMEM((WIN, 8, rows), f32),
            pltpu.VMEM((WIN + 1, rows, rows), f32),
            pltpu.VMEM((nmp - 1, WIN + 1, share, rows), f32),
            pltpu.VMEM((WIN + 2, rows, rows), bf),
            pltpu.VMEM((WIN, share, rows), bf),
            pltpu.VMEM((WIN, rows, rows), bf),
            pltpu.VMEM((nst + 1, 8, 128), f32),
            pltpu.VMEM((nst, 8, 128), f32),
            dma((4, CHUNKS)), dma((WIN, CHUNKS)),
            dma((4, CHUNKS)), dma((WIN, CHUNKS)),
            dma((WIN,)), dma((WIN,)),
            dma((nmp - 1, WIN + 1)), dma((nmp - 1, WIN + 1)),
            dma((nmp,)), dma((nmp,)),
            dma((WIN,)), dma((WIN,)),
            dma((nmp,)), dma((nmp,)),
            dma((nst,)), dma((nst,)),
        ],
        compiler_params=pltpu.CompilerParams(
            collective_id=0, has_side_effects=True, vmem_limit_bytes=56 * 1024 * 1024),
    )(query, passage, ps, qs, meta)
    return loss.reshape(()), gq, gp


def solution(mesh):
    return jax.shard_map(
        functools.partial(local, mesh.shape["dp"], mesh.shape["mp"]),
        mesh=mesh,
        in_specs=(P("dp", "mp"), P("dp", "mp"), P("dp"), P("dp"), P("dp", None), P()),
        out_specs=(P(), P("dp", "mp"), P("dp", "mp")),
        check_vma=False,
    )
```

```python
import functools
import math

import jax
import jax.numpy as jnp
from jax import lax
from jax.experimental import pallas as pl
from jax.experimental.pallas import tpu as pltpu
from jax.sharding import PartitionSpec as P

WIN = 3
CHUNKS = 4
GROUP = 32
MESH = pl.DeviceIdType.MESH


def kernel(ndp, nmp, inv, q_ref, p_ref, ps_ref, qs_ref, meta_ref,
           gq_ref, gp_ref, loss_ref,
           pbuf, qbuf, psbuf, raw, inbox, weights, rw_out, rw_in, acc, lsum, lin,
           p_ss, p_rs, q_ss, q_rs, sc_ss, sc_rs, t_ss, t_rs, k_ss, k_rs,
           d_ss, d_rs, g_ss, g_rs, l_ss, l_rs):
    d = lax.axis_index("dp")
    m = lax.axis_index("mp")
    rows, width = q_ref.shape
    share = rows // nmp
    step = rows // CHUNKS

    def at_dp(delta):
        return (lax.rem(d + delta + ndp, ndp), m)

    def at_mp(delta):
        return (d, lax.rem(m + delta, nmp))

    def flip(index, bit):
        return index + bit - 2 * bit * lax.rem(index // bit, 2)

    def rows_of(block):
        return pl.ds(pl.multiple_of(block * share, share), share)

    even = lax.rem(d, 2) == 0
    odd = lax.rem(d, 2) == 1
    partner = (flip(d, 1), m)
    mp_bits = [1 << b for b in range(nmp.bit_length() - 1)]
    dp_bits = [1 << b for b in range(ndp.bit_length() - 1)]

    peers = [at_dp(s * k) for k in range(1, WIN + 1) for s in (1, -1)]
    peers += [at_mp(j) for j in range(1, nmp)]
    peers += [(flip(d, b), m) for b in dp_bits if b > WIN]
    barrier = pltpu.get_barrier_semaphore()
    for peer in peers:
        pl.semaphore_signal(barrier, inc=1, device_id=peer, device_id_type=MESH)
    pl.semaphore_wait(barrier, len(peers))

    def copy(src, dst, ssem, rsem, dev):
        return pltpu.make_async_remote_copy(
            src_ref=src, dst_ref=dst, send_sem=ssem, recv_sem=rsem,
            device_id=dev, device_id_type=MESH)

    class Stream:
        def __init__(self, own, buf, ss, rs, dest):
            self.own, self.buf, self.ss, self.rs, self.dest = own, buf, ss, rs, dest

        def cut(self, c):
            return pl.ds(c * step, step)

        def direct(self, c):
            s = self.cut(c)
            return copy(self.own.at[s], self.buf.at[1, s], self.ss.at[0, c], self.rs.at[1, c], self.dest)

        def near_relay(self, c):
            s = self.cut(c)
            return copy(self.buf.at[1, s], self.buf.at[0, s], self.ss.at[1, c], self.rs.at[0, c], partner)

        def near_own(self, c):
            s = self.cut(c)
            return copy(self.own.at[s], self.buf.at[0, s], self.ss.at[1, c], self.rs.at[0, c], partner)

        def far_near(self, c):
            s = self.cut(c)
            return copy(self.buf.at[1, s], self.buf.at[2, s], self.ss.at[2, c], self.rs.at[2, c], partner)

        def far_next(self, c):
            s = self.cut(c)
            return copy(self.buf.at[0, s], self.buf.at[2, s], self.ss.at[3, c], self.rs.at[2, c], self.dest)

        def arrived(self, slot, c):
            s = self.cut(c)
            copy(self.buf.at[slot, s], self.buf.at[slot, s], self.ss.at[0, c], self.rs.at[slot, c], partner).wait_recv()

        def start_own(self, is_b):
            for c in range(CHUNKS):
                self.direct(c).start()

            @pl.when(is_b)
            def _():
                for c in range(CHUNKS):
                    self.near_own(c).start()

        def relay_two(self, is_b):
            for c in range(CHUNKS):
                self.arrived(1, c)

                @pl.when(is_b)
                def _():
                    self.far_near(c).start()

                @pl.when(jnp.logical_not(is_b))
                def _():
                    self.near_relay(c).start()

        def relay_one(self, is_b):
            for c in range(CHUNKS):
                self.arrived(0, c)

                @pl.when(is_b)
                def _():
                    self.far_next(c).start()

        def relay_all(self, is_b):
            for c in range(CHUNKS):
                self.arrived(1, c)

                @pl.when(is_b)
                def _():
                    self.far_near(c).start()
                    self.arrived(0, c)
                    self.far_next(c).start()

                @pl.when(jnp.logical_not(is_b))
                def _():
                    self.near_relay(c).start()
                    self.arrived(0, c)

        def finish(self, is_b):
            for c in range(CHUNKS):
                self.direct(c).wait_send()

                @pl.when(is_b)
                def _():
                    self.near_own(c).wait_send()
                    self.far_near(c).wait_send()
                    self.far_next(c).wait_send()

                @pl.when(jnp.logical_not(is_b))
                def _():
                    self.near_relay(c).wait_send()

    ps = Stream(p_ref, pbuf, p_ss, p_rs, at_dp(-2))
    qs = Stream(q_ref, qbuf, q_ss, q_rs, at_dp(2))

    def scale_copy(k):
        return copy(ps_ref, psbuf.at[k - 1], sc_ss.at[k - 1], sc_rs.at[k - 1], at_dp(-k))

    for k in range(1, WIN + 1):
        scale_copy(k).start()
    ps.start_own(odd)

    def across(s):
        block = m
        for b in mp_bits:
            if s & b:
                block = flip(block, b)
        return rows_of(block)

    def tile_copy(k, s):
        return copy(raw.at[k, across(s)], inbox.at[s - 1, k],
                    t_ss.at[s - 1, k], t_rs.at[s - 1, k], (d, flip(m, s & -s)))

    def tile_next(k):
        for bit in mp_bits[1:]:
            for s in range(bit, nmp, 2 * bit):
                for b in mp_bits:
                    if b < bit:
                        tile_copy(k, s | b).wait_recv()
                        raw[k, across(s), :] += inbox[(s | b) - 1, k]
                tile_copy(k, s).start()

    def tile(k):
        keys = p_ref if k == 0 else pbuf.at[k - 1]

        @pl.loop(0, nmp)
        def _(r):
            at = rows_of(r)
            raw[k, at, :] = lax.dot_general(
                q_ref[at, :], keys[...], (((1,), (1,)), ((), ())),
                preferred_element_type=jnp.float32)
        for s in range(1, nmp, 2):
            tile_copy(k, s).start()

    tile(0)
    tile_next(0)
    ps.relay_two(odd)
    qs.start_own(even)
    ps.relay_one(odd)
    tile(2)
    tile(1)
    tile_next(2)
    tile_next(1)
    qs.relay_two(even)
    for c in range(CHUNKS):
        ps.arrived(2, c)
    tile(3)
    tile_next(3)
    for k in range(1, WIN + 1):
        scale_copy(k).wait_recv()
    for k in (0, 2, 1, 3):
        for b in mp_bits:
            tile_copy(k, b).wait_recv()

    lsum[...] = jnp.zeros_like(lsum)

    @pl.loop(0, share // GROUP)
    def _(g):
        low = pl.multiple_of(g * GROUP, GROUP)
        here = pl.ds(low, GROUP)
        whole = pl.ds(pl.multiple_of(m * share + low, GROUP), GROUP)
        row_scale = qs_ref[whole, :]
        cols = lax.broadcasted_iota(jnp.int32, (GROUP, rows), 1)
        ids = lax.broadcasted_iota(jnp.int32, (GROUP, rows), 0) + (m * share + low)
        diagonal = cols == ids
        valid = ids[:, 0:1] < meta_ref[0]
        key_scale = [ps_ref[0:1, :]] + [psbuf[k, 0:1, :] for k in range(WIN)]
        scores = []
        for k in range(WIN + 1):
            s = raw[k, whole, :]
            for b in mp_bits:
                s = s + inbox[b - 1, k, here, :]
            scores.append(s * (row_scale * inv) * key_scale[k])
        masked = [jnp.where(cols < meta_ref[k], scores[k], -jnp.inf) for k in range(WIN + 1)]
        top = functools.reduce(jnp.maximum, [jnp.max(x, axis=1, keepdims=True) for x in masked])
        exps = [jnp.exp(x - top) for x in masked]
        total = sum(jnp.sum(x, axis=1, keepdims=True) for x in exps)
        lse = top + jnp.log(total)
        positive = jnp.sum(jnp.where(diagonal, scores[0], 0.0), axis=1, keepdims=True)
        lost = jnp.sum(jnp.where(valid, lse - positive, 0.0), axis=0, keepdims=True)
        lsum[0] = lsum[0] + lost
        for k in range(WIN + 1):
            grad = exps[k] / total
            if k == 0:
                grad = grad - diagonal.astype(jnp.float32)
            grad = jnp.where(valid, grad, 0.0)
            weights[k, whole, :] = (grad * key_scale[k]).astype(jnp.bfloat16)
            if k == 0:
                weights[WIN + 1, whole, :] = (grad * row_scale).astype(jnp.bfloat16)
            else:
                rw_out[k - 1, here, :] = (grad * row_scale).astype(jnp.bfloat16)

    def dispatch(k):
        return copy(rw_out.at[k - 1], rw_in.at[k - 1, rows_of(m)], d_ss.at[k - 1], d_rs.at[k - 1], at_dp(k))

    for k in range(1, WIN + 1):
        dispatch(k).start()

    class Gather:
        def __init__(self, buf, ss, rs):
            self.buf, self.ss, self.rs = buf, ss, rs
            known = [0]
            self.steps = []
            for bit in reversed(mp_bits):
                self.steps += [(s, bit) for s in known]
                known = known + [s ^ bit for s in known]
            self.steps.sort(key=lambda t: t[0])
            self.got = set()

        def hop(self, s, bit):
            block = m
            for b in mp_bits:
                if s & b:
                    block = flip(block, b)
            part = self.buf.at[:, rows_of(block)]
            return copy(part, part, self.ss.at[s ^ bit], self.rs.at[s ^ bit], (d, flip(m, bit)))

        def take(self, s):
            if s and s not in self.got:
                self.got.add(s)
                block = m
                for b in mp_bits:
                    if s & b:
                        block = flip(block, b)
                part = self.buf.at[:, rows_of(block)]
                copy(part, part, self.ss.at[s], self.rs.at[s], (d, flip(m, 1))).wait_recv()

        def begin(self):
            for s, bit in self.steps:
                if s == 0:
                    self.hop(s, bit).start()

        def rest(self):
            for s, bit in self.steps:
                if s:
                    self.take(s)
                    self.hop(s, bit).start()

        def all(self):
            for s in range(1, nmp):
                self.take(s)

        def finish(self):
            for s, bit in self.steps:
                self.hop(s, bit).wait_send()

    local = Gather(weights, k_ss, k_rs)
    foreign = Gather(rw_in, g_ss, g_rs)
    stages = [(d, flip(m, b)) for b in mp_bits] + [(flip(d, b), m) for b in dp_bits]

    def loss_copy(i):
        return copy(lsum.at[i], lin.at[i], l_ss.at[i], l_rs.at[i], stages[i])

    def loss_step(i):
        if i:
            loss_copy(i - 1).wait_recv()
            lsum[i] = lsum[i - 1] + lin[i - 1]
        if i < len(stages):
            loss_copy(i).start()

    local.begin()
    loss_step(0)
    qs.relay_one(even)
    loss_step(1)
    for k in range(1, WIN + 1):
        dispatch(k).wait_recv()
    foreign.begin()
    loss_step(2)
    local.rest()
    loss_step(3)
    local.all()

    @pl.loop(0, nmp)
    def _(r):
        at = rows_of(r)
        out = jnp.dot(weights[0, at, :], p_ref[...], preferred_element_type=jnp.float32)
        for k in range(WIN):
            out = out + jnp.dot(weights[k + 1, at, :], pbuf[k], preferred_element_type=jnp.float32)
        gq_ref[at, :] = out.astype(jnp.bfloat16)

    loss_step(4)
    foreign.rest()
    def back(w, x):
        return lax.dot_general(w, x, (((0,), (0,)), ((), ())), preferred_element_type=jnp.float32)

    foreign.all()
    for i in range(5, len(stages) + 1):
        loss_step(i)
    loss_ref[...] = lsum[len(stages), 0:1, 0:1] / meta_ref[WIN + 1].astype(jnp.float32)
    jc = 128

    @pl.loop(0, rows // jc)
    def _(t):
        at = pl.ds(pl.multiple_of(t * jc, jc), jc)
        out = back(weights[WIN + 1, :, at], q_ref[...])
        for k in range(WIN - 1):
            out = out + back(rw_in[k, :, at], qbuf[k])
        acc[at, :] = out

    for c in range(CHUNKS):
        qs.arrived(2, c)

    @pl.loop(0, rows // jc)
    def _(t):
        at = pl.ds(pl.multiple_of(t * jc, jc), jc)
        out = acc[at, :] + back(rw_in[WIN - 1, :, at], qbuf[WIN - 1])
        gp_ref[at, :] = out.astype(jnp.bfloat16)

    ps.finish(odd)
    qs.finish(even)
    for k in range(1, WIN + 1):
        scale_copy(k).wait_send()
        dispatch(k).wait_send()
    for k in range(WIN + 1):
        for j in range(1, nmp):
            tile_copy(k, j).wait_send()
    local.finish()
    foreign.finish()
    for i in range(len(stages)):
        loss_copy(i).wait_send()


def local(ndp, nmp, query, passage, query_scale, passage_scale, partners, counts):
    rows, width = query.shape
    inv = 1.0 / math.sqrt(width * nmp)
    share = rows // nmp
    mine = lax.axis_index("dp")
    ids = jnp.arange(counts.shape[0], dtype=jnp.int32)
    offsets = jnp.arange(WIN + 1, dtype=jnp.int32)
    near = (mine + offsets) % ndp
    key_counts = jnp.sum(jnp.where(ids[None, :] == near[:, None], counts[None, :], 0), axis=1)
    live = (offsets == 0) | jnp.any(partners[0][None, :] == offsets[:, None], axis=1)
    meta = jnp.concatenate([jnp.where(live, key_counts, 0), jnp.sum(counts)[None]]).astype(jnp.int32)
    ps = jnp.broadcast_to(passage_scale.astype(jnp.float32)[None, :], (8, rows))
    qs = query_scale.astype(jnp.float32)[:, None]
    nst = (ndp * nmp).bit_length() - 1
    bf, f32 = jnp.bfloat16, jnp.float32
    dma = pltpu.SemaphoreType.DMA
    vm = pl.BlockSpec(memory_space=pltpu.VMEM)
    gq, gp, loss = pl.pallas_call(
        functools.partial(kernel, ndp, nmp, inv),
        out_shape=[
            jax.ShapeDtypeStruct((rows, width), bf),
            jax.ShapeDtypeStruct((rows, width), bf),
            jax.ShapeDtypeStruct((1, 1), f32),
        ],
        in_specs=[vm] * 4 + [pl.BlockSpec(memory_space=pltpu.SMEM)],
        out_specs=[vm] * 3,
        scratch_shapes=[
            pltpu.VMEM((WIN, rows, width), bf),
            pltpu.VMEM((WIN, rows, width), bf),
            pltpu.VMEM((WIN, 8, rows), f32),
            pltpu.VMEM((WIN + 1, rows, rows), f32),
            pltpu.VMEM((nmp - 1, WIN + 1, share, rows), f32),
            pltpu.VMEM((WIN + 2, rows, rows), bf),
            pltpu.VMEM((WIN, share, rows), bf),
            pltpu.VMEM((WIN, rows, rows), bf),
            pltpu.VMEM((rows, width), f32),
            pltpu.VMEM((nst + 1, 8, 128), f32),
            pltpu.VMEM((nst, 8, 128), f32),
            dma((4, CHUNKS)), dma((WIN, CHUNKS)),
            dma((4, CHUNKS)), dma((WIN, CHUNKS)),
            dma((WIN,)), dma((WIN,)),
            dma((nmp - 1, WIN + 1)), dma((nmp - 1, WIN + 1)),
            dma((nmp,)), dma((nmp,)),
            dma((WIN,)), dma((WIN,)),
            dma((nmp,)), dma((nmp,)),
            dma((nst,)), dma((nst,)),
        ],
        compiler_params=pltpu.CompilerParams(
            collective_id=0, has_side_effects=True, vmem_limit_bytes=56 * 1024 * 1024),
    )(query, passage, ps, qs, meta)
    return loss.reshape(()), gq, gp


def solution(mesh):
    return jax.shard_map(
        functools.partial(local, mesh.shape["dp"], mesh.shape["mp"]),
        mesh=mesh,
        in_specs=(P("dp", "mp"), P("dp", "mp"), P("dp"), P("dp"), P("dp", None), P()),
        out_specs=(P(), P("dp", "mp"), P("dp", "mp")),
        check_vma=False,
    )
```
